256 devices in a mesh: dp: 4 (over y), row: 16 (over z, core), col: 4 (over x).
Axes of the slice: x: 4, y: 4, z: 8, core: 2. Of those that a mesh axis runs over, the one named last changes fastest.
Arguments:
- tokens: bfloat16 [1024, 4096], P('dp', 'row'), may hold values from -6 to 6
- embed_noise: bfloat16 [1024, 4096], P('dp', 'row'), may hold values from -1 to 1
- cotangent: bfloat16 [1024, 4096], P('dp', 'row'), may hold values from -1.5 to 1.5
- gate_weight: bfloat16 [4096, 14336], P('row', 'col'), may hold values from -0.09375 to 0.09375
- up_weight: bfloat16 [4096, 14336], P('row', 'col'), may hold values from -0.09375 to 0.09375
- down_weight: bfloat16 [14336, 4096], P('col', 'row'), may hold values from -0.046875 to 0.046875
- lengths: int32 [4, 8], P('dp'), may hold values from 1 to 128, 256 in all within a row
- pad_mask: int32 [1024], P('dp'), may hold values 0 or 1
Outputs:
- grad_tokens: bfloat16 [1024, 4096], P('dp', 'row')
- grad_gate: float32 [4096, 4, 3584], P('row', 'col', 'dp')
- grad_up: float32 [4096, 4, 3584], P('row', 'col', 'dp')
- grad_down: float32 [4, 3584, 4096], P('col', 'dp', 'row')
The draws below stay inside these ranges and needn't reach their ends.
Inputs may be any that keep to these rules, and one draw needn't show every extreme that they name: Each data group's 8 lengths sum to 256.
All inputs are finite; a program needn't handle non-finite values. No bound on the sum of `pad_mask` on one device may be relied on, other than what follows from the above.
Results may differ from the reference program's by a relative error of at most 0.0062.
Values may be sent and summed in bfloat16 or wider, within the bound.
No kernel may reach another device: no remote copies, remote signals or barrier semaphores. Data moves between devices by JAX's collectives and lax.ppermute only.
A program may use at most 128 MiB of HBM per device.

```python
import math
import jax
import jax.numpy as jnp
import numpy as np
from jax import lax

D = 4096
FF = 14336
TOK_GROUP = 256
SEQS = 8
TOKENS = 1024
N_DP = 4
N_COL = 4


def place_ends(array, own_key, low, top_value):
    longest = array.shape.index(max(array.shape))
    spots = []
    for shift in (0, 1):
        where = [jax.random.randint(jax.random.fold_in(own_key, axis), (), 0, length) for axis, length in enumerate(array.shape)]
        where[longest] = (where[longest] + shift) % array.shape[longest]
        spots.append(tuple(where))
    return array.at[spots[0]].set(low).at[spots[1]].set(top_value)


def level_of(stream_key, extent, cuts, least, high):
    level = 1.0
    for dim, blocks in cuts:
        draws = jax.random.uniform(jax.random.fold_in(jax.random.fold_in(stream_key, 6), dim), (blocks,), jnp.float32, least / len(cuts), high / len(cuts))
        level = level * jnp.repeat(jnp.exp(draws), extent[dim] // blocks).reshape((-1,) + (1,) * (len(extent) - 1 - dim))
    return level


def split_up(count, total, limit, slope):
    weights = [(1 << 20) // math.isqrt(standing ** slope) + 1 for standing in range(2, count + 1)]
    rest, holding = total - limit - (count - 1), [1] * (count - 1)
    while rest > 0:
        free = [i for i in range(count - 1) if holding[i] < limit]
        mass, remaining = sum([weights[i] for i in free]), rest
        for i in free:
            addition = min(limit - holding[i], max(1, remaining * weights[i] // mass), rest)
            holding[i] = holding[i] + addition
            rest = rest - addition
    return np.array([limit] + holding)


def ragged_sizes(own_key, number_of, total, limit, lean):
    if number_of == 2:
        one = jax.random.randint(own_key, (), max(1, total - limit), min(limit, total - 1) + 1)
        return jnp.stack([one, total - one])
    sizes = jnp.asarray(split_up(number_of, total, limit, lean), jnp.int32)
    pairs = (number_of - 1) // 2
    donor, receiver = sizes[1:1 + 2 * pairs:2], sizes[2:2 + 2 * pairs:2]
    room = jnp.minimum(donor - 1, limit - receiver)
    shifted = jax.random.randint(jax.random.fold_in(own_key, 1), (pairs,), 0, 1 << 20) % (room + 1)
    sizes = sizes.at[1:1 + 2 * pairs:2].set(donor - shifted).at[2:2 + 2 * pairs:2].set(receiver + shifted)
    return sizes[jax.random.permutation(jax.random.fold_in(own_key, 2), number_of)]


def normal_values(key, shape, spread, limit, shards=(), held_as=jnp.bfloat16):
    loudness = level_of(key, shape, shards, -0.22, 0.18) if shards else 1.0
    result = jax.random.normal(key, shape, jnp.float32) * spread * loudness
    return jnp.minimum(jnp.maximum(result, -limit), limit).astype(held_as)


def setup_inputs(seed: int = 0) -> dict:
    keys = jax.random.split(jax.random.key(seed), 9)
    return {
        "tokens": normal_values(keys[0], (TOKENS, D), 1.0, 6.0, ((0, 4), (1, 16))),
        "embed_noise": jnp.clip(jax.random.uniform(keys[1], (TOKENS, D), jnp.float32, -1.0, 1.0) * level_of(keys[1], (TOKENS, D), ((0, 4), (1, 16)), -0.4, 0.0), -1.0, 1.0).astype(jnp.bfloat16),
        "cotangent": normal_values(keys[2], (TOKENS, D), 0.25, 1.5, ((0, 4), (1, 16))),
        "gate_weight": normal_values(keys[3], (D, FF), D ** -0.5, 0.09375, ((0, 16), (1, 4))),
        "up_weight": normal_values(keys[4], (D, FF), D ** -0.5, 0.09375, ((0, 16), (1, 4))),
        "down_weight": normal_values(keys[5], (FF, D), FF ** -0.5, 0.046875, ((0, 4), (1, 16))),
        "lengths": jax.vmap(lambda own: ragged_sizes(own, SEQS, TOK_GROUP, TOK_GROUP // 2, 2))(jax.random.split(keys[6], N_DP)).reshape((N_DP, SEQS)).astype(jnp.int32),
        "pad_mask": place_ends((jax.random.randint(keys[7], (TOKENS,), 0, 4) < 3).astype(jnp.int32), jax.random.fold_in(keys[7], 1), 0, 1),
    }


def token_lengths(lengths):
    seq_ends = jnp.cumsum(lengths, axis=1, dtype=jnp.int32)
    seq_starts = seq_ends - lengths
    indices = jnp.arange(TOKENS, dtype=jnp.int32)
    groups = indices // TOK_GROUP
    positions = indices - groups * TOK_GROUP
    within = (positions[:, None] >= seq_starts[groups]) & (positions[:, None] < seq_ends[groups])
    return lax.optimization_barrier(jnp.sum(jnp.where(within, lengths[groups], 0), axis=1, dtype=jnp.int32))

def reference(tokens, embed_noise, cotangent, gate_weight, up_weight, down_weight, lengths, pad_mask):
    seq_length = token_lengths(lengths)
    noise_scale = 4.0 / jnp.sqrt(seq_length.astype(jnp.float32))
    noisy_tokens = (tokens.astype(jnp.float32) + noise_scale[:, None] * embed_noise.astype(jnp.float32)).astype(jnp.bfloat16)
    grad_out = cotangent * pad_mask[:, None].astype(jnp.bfloat16)
    gate_act = jnp.dot(noisy_tokens, gate_weight, preferred_element_type=jnp.float32)
    up_act = jnp.dot(noisy_tokens, up_weight, preferred_element_type=jnp.float32)
    sigmoid_gate = jax.nn.sigmoid(gate_act)
    silu_gate = gate_act * sigmoid_gate
    hidden = (silu_gate * up_act).astype(jnp.bfloat16)
    d_hidden = jnp.dot(grad_out, down_weight.T, preferred_element_type=jnp.float32)
    grad_gate_act = (d_hidden * up_act * sigmoid_gate * (1.0 + gate_act * (1.0 - sigmoid_gate))).astype(jnp.bfloat16)
    grad_up_act = (d_hidden * silu_gate).astype(jnp.bfloat16)
    grad_tokens = (jnp.dot(grad_gate_act, gate_weight.T, preferred_element_type=jnp.float32) + jnp.dot(grad_up_act, up_weight.T, preferred_element_type=jnp.float32)).astype(jnp.bfloat16)
    grad_gate = jnp.dot(noisy_tokens.T, grad_gate_act, preferred_element_type=jnp.float32).reshape(D, N_COL, FF // N_COL)
    grad_up = jnp.dot(noisy_tokens.T, grad_up_act, preferred_element_type=jnp.float32).reshape(D, N_COL, FF // N_COL)
    grad_down = jnp.dot(hidden.T, grad_out, preferred_element_type=jnp.float32).reshape(N_COL, FF // N_COL, D)
    return (grad_tokens, grad_gate, grad_up, grad_down)
```

```python
import jax
import jax.numpy as jnp
from jax import lax
from jax.sharding import PartitionSpec as P

F32 = jnp.float32
BF16 = jnp.bfloat16
ZS = 8
NY = 4


def dot(a, b):
    return lax.dot_general(a, b, (((1,), (0,)), ((), ())), preferred_element_type=F32)


def contract_first(left, right):
    return lax.dot_general(left, right, (((0,), (0,)), ((), ())), preferred_element_type=F32)


def contract_last(left, right):
    return lax.dot_general(left, right, (((1,), (1,)), ((), ())), preferred_element_type=F32)


def shift(x, axis, n, by):
    return lax.ppermute(x, axis, [(i, (i + by) % n) for i in range(n)])


def swap_core(x):
    return lax.ppermute(x, "row", [(i, i ^ 1) for i in range(2 * ZS)])


def up_z(x):
    return shift(x, "row", 2 * ZS, 2)


def down_z(x):
    return shift(x, "row", 2 * ZS, -2)


def per_device(
    tokens, embed_noise, cotangent, gate_weight, up_weight, down_weight, lengths, pad_mask
):
    rows, feats = tokens.shape
    ff = gate_weight.shape[1] // NY
    half = rows // 2
    sub = half // ZS
    blk = NY * sub
    dp = lax.axis_index("dp")
    row = lax.axis_index("row")
    core = row % 2
    z = row // 2

    gate_own = lax.dynamic_slice(gate_weight, (0, dp * ff), (feats, ff))
    up_own = lax.dynamic_slice(up_weight, (0, dp * ff), (feats, ff))
    down_own = lax.dynamic_slice(down_weight, (dp * ff, 0), (ff, feats))
    gu_own = jnp.concatenate([gate_own, up_own], axis=1)
    gu = jnp.concatenate([gu_own, swap_core(gu_own)], axis=0)
    down = jnp.concatenate([down_own, swap_core(down_own)], axis=1)

    positions = jnp.arange(rows, dtype=jnp.int32)
    seq_lengths = lengths[0]
    seq_ends = jnp.cumsum(seq_lengths, dtype=jnp.int32)
    seq_starts = seq_ends - seq_lengths
    within = (positions[:, None] >= seq_starts[None, :]) & (positions[:, None] < seq_ends[None, :])
    seq_length = jnp.sum(jnp.where(within, seq_lengths[None, :], 0), axis=1, dtype=jnp.int32)
    noise_scale = 4.0 / jnp.sqrt(seq_length.astype(F32))
    noisy = (tokens.astype(F32) + noise_scale[:, None] * embed_noise.astype(F32)).astype(BF16)
    grad_out = cotangent * pad_mask[:, None].astype(BF16)
    both = jnp.concatenate([noisy, grad_out], axis=1).reshape(2, half, 2 * feats)

    def rolled(h):
        part = lax.dynamic_index_in_dim(both, h, 0, keepdims=False)
        return lax.dynamic_slice(
            jnp.concatenate([part, part], axis=0), (z * sub, 0), (half, 2 * feats)
        )

    mine = rolled(core)
    theirs = swap_core(rolled(1 - core))
    local = jnp.concatenate(
        [mine[:, :feats], theirs[:, :feats], mine[:, feats:], theirs[:, feats:]], axis=1
    )

    from_up = shift(local, "dp", NY, -1)
    from_down = shift(local, "dp", NY, 1)
    far_a = shift(from_up[: half // 2], "dp", NY, -1)
    far_b = shift(from_down[half // 2 :], "dp", NY, 1)
    far = jnp.concatenate([far_a, far_b], axis=0)
    x = jnp.stack(
        [g.reshape(ZS, sub, 4 * feats) for g in (local, from_up, from_down, far)], axis=1
    ).reshape(ZS, blk, 4 * feats)
    xn = x[:, :, : 2 * feats]
    xg = x[:, :, 2 * feats :]

    def partial(j):
        j = j % ZS
        return jnp.concatenate([dot(xn[j], gu), contract_last(xg[j], down)], axis=1)

    hb = blk // 2
    p4 = partial(4).astype(BF16)
    dn = down_z(p4[:hb])
    upm = up_z(p4[hb:])
    pd, pu = partial(-3), partial(3)
    dn = jnp.concatenate([pd[:hb] + dn.astype(F32), pd[hb:]], axis=0).astype(BF16)
    upm = jnp.concatenate([pu[:hb], pu[hb:] + upm.astype(F32)], axis=0).astype(BF16)
    dn, upm = down_z(dn), up_z(upm)
    for j in (2, 1):
        dn = (partial(-j) + dn.astype(F32)).astype(BF16)
        upm = (partial(j) + upm.astype(F32)).astype(BF16)
        dn, upm = down_z(dn), up_z(upm)
    summed = partial(0) + (dn.astype(F32) + upm.astype(F32))

    gate_act = summed[:, :ff]
    up_act = summed[:, ff : 2 * ff]
    d_hidden = summed[:, 2 * ff :]
    sig = jax.nn.sigmoid(gate_act)
    silu = gate_act * sig
    hidden = (silu * up_act).astype(BF16)
    d_gate = (d_hidden * up_act * sig * (1.0 + gate_act * (1.0 - sig))).astype(BF16)
    d_up = (d_hidden * silu).astype(BF16)
    own = jnp.concatenate([d_gate, d_up, hidden], axis=1)

    blocks = [None] * ZS
    blocks[0] = own
    a, b = own, own
    for j in (1, 2, 3):
        a, b = down_z(a), up_z(b)
        blocks[j] = a
        blocks[ZS - j] = b
    blocks[4] = jnp.concatenate([down_z(a[:hb]), up_z(b[hb:])], axis=0)
    act = jnp.concatenate(blocks, axis=0)
    d_gu = act[:, : 2 * ff]
    hid = act[:, 2 * ff :]
    xn_all = xn.reshape(ZS * blk, 2 * feats)
    xg_all = xg.reshape(ZS * blk, 2 * feats)

    t = contract_last(d_gu, gu).reshape(ZS, NY, sub, 2 * feats)
    t0, t1, t2, t3 = (t[:, q].reshape(half, 2 * feats) for q in range(NY))
    hh = half // 2
    fa = shift(t3[:hh].astype(BF16), "dp", NY, 1).astype(F32)
    fb = shift(t3[hh:].astype(BF16), "dp", NY, -1).astype(F32)
    t1 = jnp.concatenate([t1[:hh] + fa, t1[hh:]], axis=0).astype(BF16)
    t2 = jnp.concatenate([t2[:hh], t2[hh:] + fb], axis=0).astype(BF16)
    t1 = shift(t1, "dp", NY, 1)
    t2 = shift(t2, "dp", NY, -1)
    ysum = (t0 + (t1.astype(F32) + t2.astype(F32))).astype(BF16)
    xp = shift(ysum, "col", NY, 1)
    xm = shift(ysum, "col", NY, -1)
    xo = shift(ysum, "col", NY, 2)
    total = (
        (ysum.astype(F32) + xo.astype(F32)) + (xp.astype(F32) + xm.astype(F32))
    ).astype(BF16)
    mine_t = total[:, :feats]
    theirs_t = swap_core(total[:, feats:])
    first = jnp.where(core == 0, mine_t, theirs_t)
    second = jnp.where(core == 0, theirs_t, mine_t)

    def unrolled(v):
        return lax.dynamic_slice(
            jnp.concatenate([v, v], axis=0), (((ZS - z) % ZS) * sub, 0), (half, feats)
        )

    grad_tokens = jnp.concatenate([unrolled(first), unrolled(second)], axis=0)

    g = contract_first(xn_all, d_gu)
    w = contract_first(hid, xg_all)
    g_own = g[:feats] + swap_core(g[feats:].astype(BF16)).astype(F32)
    w_own = w[:, :feats] + swap_core(w[:, feats:].astype(BF16)).astype(F32)
    return (
        grad_tokens,
        g_own[:, None, :ff],
        g_own[:, None, ff:],
        w_own[None],
    )


def solution(mesh):
    in_specs = (
        P("dp", "row"),
        P("dp", "row"),
        P("dp", "row"),
        P("row", "col"),
        P("row", "col"),
        P("col", "row"),
        P("dp", None),
        P("dp"),
    )
    out_specs = (
        P("dp", "row"),
        P("row", "col", "dp"),
        P("row", "col", "dp"),
        P("col", "dp", "row"),
    )
    return jax.shard_map(
        per_device, mesh=mesh, in_specs=in_specs, out_specs=out_specs, check_vma=False
    )
```
